256 devices in a mesh: row: 8 (over y, z_lo), col: 32 (over x, z_hi, core).
Axes of the slice: x: 4, y: 4, z: 8 (z_hi: 4, z_lo: 2; z = z_hi * 2 + z_lo), core: 2. Of those that a mesh axis runs over, the one named last changes fastest.
Arguments:
- matrix: float32 [16384, 16384], P('row', 'col'), may hold values from -6 to 6
- reflectors: float32 [16384, 256], P(('row', 'col')), may hold values from -0.046875 to 0.046875
- factor: float32 [256, 256], replicated, may hold values from -0.375 to 0.375
Outputs:
- updated: float32 [16384, 16384], P('row', 'col')
- correction: float32 [16384, 256], P(('row', 'col'))
The draws below stay inside these ranges and needn't reach their ends.
All inputs are finite; a program needn't handle non-finite values.
Results may differ from the reference program's by a relative error of at most 0.000078.
Values sent between devices are 32-bit elements; how exact they have to be, the bound alone decides.
No kernel may reach another device: no remote copies, remote signals or barrier semaphores. Data moves between devices by JAX's collectives and lax.ppermute only.
A program may use at most 64 MiB of HBM per device.

```python
import math
import jax
import jax.numpy as jnp
from jax import lax

N = 16384
B = 256


def draw_matrix(key, part):
    normal_draw = jax.random.normal(key, (N, N), jnp.float32)
    symmetric = (normal_draw + normal_draw.T) * math.sqrt(0.5)
    return jnp.clip(symmetric, -6.0, 6.0)


def steps_of(stream_key, extent, cuts, least, high):
    gain = 1.0
    for position, shards_of in cuts:
        heights = jax.random.uniform(jax.random.fold_in(jax.random.fold_in(stream_key, 6), position), (shards_of,), jnp.float32, least / len(cuts), high / len(cuts))
        gain = gain * jnp.repeat(jnp.exp(heights), extent[position] // shards_of).reshape((-1,) + (1,) * (len(extent) - 1 - position))
    return gain


def normal_values(key, extent, spread, reach, split=(), kind=jnp.bfloat16):
    drawn = spread * jax.random.normal(key, extent, jnp.float32)
    if split:
        drawn = drawn * steps_of(key, extent, split, -0.22, 0.18)
    return jnp.clip(drawn, -reach, reach).astype(kind)


def setup_inputs(seed: int = 0) -> dict:
    streams_of = jax.random.split(jax.random.key(seed), 4)
    matrix = draw_matrix(jax.random.fold_in(streams_of[3], 71), 0)
    reflectors = normal_values(streams_of[1], (N, B), N ** -0.5, 0.046875, ((0, 256),), jnp.float32)
    factor = normal_values(streams_of[2], (B, B), B ** -0.5, 0.375, (), jnp.float32)
    return dict(matrix=matrix, reflectors=reflectors, factor=factor)


def mult(left, right):
    return jnp.dot(left, right, precision=lax.Precision.HIGHEST, preferred_element_type=jnp.float32)


def reference(matrix, reflectors, factor):
    image = mult(matrix, reflectors)
    gram_matrix = mult(reflectors.T, image)
    inner = mult(mult(factor.T, gram_matrix), factor)
    correction = mult(image, factor) - 0.5 * mult(reflectors, inner)
    updated = matrix - mult(reflectors, correction.T) - mult(correction, reflectors.T)
    return updated, correction
```

```python
import jax
import jax.numpy as jnp
from jax import lax
from jax.sharding import Mesh
from jax.sharding import PartitionSpec as P

ROW = ("y", "zl")
COL = ("x", "zh", "k")
ALL = ROW + COL
SIZES = (4, 2, 4, 4, 2)


def mm(left, right, ld, rd, precision=lax.Precision.HIGH):
    return lax.dot_general(
        left, right, (((ld,), (rd,)), ((), ())), precision=precision, preferred_element_type=jnp.float32
    )


def exact(left, right, ld, rd):
    return mm(left, right, ld, rd, lax.Precision.HIGHEST)


def shift(n, s):
    return [(i, (i + s) % n) for i in range(n)]


def to_cols():
    return [(8 * c + r, 32 * r + c) for r in range(8) for c in range(32)]


def to_rows(s):
    def moved(d):
        rest, k = divmod(d, 2)
        rest, zh = divmod(rest, 4)
        return (rest * 4 + (zh + s) % 4) * 2 + k

    return [(32 * r + c, moved(8 * c + r)) for r in range(8) for c in range(32)]


def place(pieces, axis, n):
    index = lax.axis_index(axis)
    whole = jnp.zeros((n,) + pieces[0].shape, pieces[0].dtype)
    for s, piece in enumerate(pieces):
        whole = lax.dynamic_update_index_in_dim(whole, piece, (index - s) % n, 0)
    return whole


def gather_x_core(zpart):
    xpart = [zpart] + [lax.ppermute(zpart, "x", shift(4, s)) for s in (1, 2, 3)]
    half = place(xpart, "x", 4)
    other = lax.ppermute(half, "k", shift(2, 1))
    mine = lax.axis_index("k") == 0
    first = jnp.where(mine, half, other)
    second = jnp.where(mine, other, half)
    return jnp.stack([first, second], axis=2).reshape(2048, 256)


def rows_in_group(chunk):
    return lax.all_to_all(jnp.broadcast_to(chunk, (8,) + chunk.shape), ROW, 0, 0, tiled=True)


def on_device(matrix, reflectors, factor):
    with jax.named_scope("v_cols"):
        vchunk = lax.ppermute(reflectors, ALL, to_cols())
    with jax.named_scope("v_rows"):
        vz = [reflectors] + [lax.ppermute(reflectors, "zh", shift(4, s)) for s in (1, 2, 3)]
        vec_rows = gather_x_core(place(vz, "zh", 4))
    with jax.named_scope("v_cols_gather"):
        vec_cols = rows_in_group(vchunk).reshape(512, 256)
    with jax.named_scope("image"):
        part = mm(matrix, vec_rows, 0, 0)
        wchunk = jnp.sum(lax.all_to_all(part.reshape(8, 64, 256), ROW, 0, 0, tiled=True), axis=0)
    with jax.named_scope("w_rows"):
        wz = [lax.ppermute(wchunk, ALL, to_rows(s)) for s in (0, 1, 2, 3)]
        img_rows = gather_x_core(place(wz, "zh", 4))
    with jax.named_scope("w_cols_gather"):
        img_cols = rows_in_group(wchunk).reshape(512, 256)
    with jax.named_scope("gram"):
        gpart = exact(vec_rows, img_rows, 0, 0)
        gblock = jnp.sum(lax.all_to_all(gpart.reshape(8, 32, 256), ROW, 0, 0, tiled=True), axis=0)
        gram = rows_in_group(gblock).reshape(256, 256)
    with jax.named_scope("small"):
        inner = exact(exact(factor, gram, 0, 0), factor, 1, 0)
        correction = exact(wz[0], factor, 1, 0) - 0.5 * exact(reflectors, inner, 1, 0)
        left_v = exact(img_cols, factor, 1, 0) - 0.5 * exact(vec_cols, inner + inner.T, 1, 0)
        left_w = exact(vec_cols, factor, 1, 1)
    with jax.named_scope("update"):
        updated = matrix - mm(vec_rows, left_v, 1, 1) - mm(img_rows, left_w, 1, 1)
    return updated, correction


def solution(mesh):
    fine = Mesh(mesh.devices.reshape(SIZES), ALL)
    return jax.shard_map(
        on_device,
        mesh=fine,
        in_specs=(P(ROW, COL), P(ALL, None), P()),
        out_specs=(P(ROW, COL), P(ALL, None)),
        check_vma=False,
    )
```
